32 devices in a mesh: batch: 4 (over x, core), hidden: 2 (over y), width: 4 (over z).
Axes of the slice: x: 2, y: 2, z: 4, core: 2. Of those that a mesh axis runs over, the one named last changes fastest.
Arguments:
- frames: bfloat16 [4, 512, 1280], P('batch', None, 'hidden'), may hold values from -6 to 6
- adapter_weight: bfloat16 [4, 1280, 16384], P(None, 'hidden', 'width'), may hold values from -0.078125 to 0.078125
- text_embed: bfloat16 [512, 16384], P('batch', 'width'), may hold values from -6 to 6
- audio_len: int32 [4], P('batch'), may hold values from 16 to 64, as said below
- text_len: int32 [4], P('batch'), may hold values from 32 to 112, as said below
- norm_gain: bfloat16 [16384], P('width'), may hold values from 0.5 to 1.5
- gate_up: bfloat16 [16384, 2, 26624], P('width', None, ('batch', 'hidden')), may hold values from -0.046875 to 0.046875
- cotangent: bfloat16 [512, 26624], P('width', ('batch', 'hidden')), may hold values from -0.59765625 to 0.59765625
Outputs:
- hidden: bfloat16 [512, 26624], P('width', ('batch', 'hidden'))
- weight_grad: float32 [4, 1280, 16384], P(None, 'hidden', 'width')
The draws below stay inside these ranges and needn't reach their ends.
Inputs may be any that keep to these rules, and one draw needn't show every extreme that they name: `audio_len`: some sequence holds exactly 16 audio positions and another exactly 64. audio_len + text_len never exceeds 128, and equals it in some sequence.
All inputs are finite; a program needn't handle non-finite values.
Results may differ from the reference program's by a relative error of at most 0.0059.
Values may be sent and summed in bfloat16 or wider, within the bound.
No kernel may reach another device: no remote copies, remote signals or barrier semaphores. Data moves between devices by JAX's collectives and lax.ppermute only.
A program may use at most 256 MiB of HBM per device.

```python
import jax
import jax.numpy as jnp
from jax import lax

D = 16384
FF = 26624
FEAT = 1280
LEN = 128
ROWS = 4
TOKENS = 512


def length_pair(key):
    folded = jax.random.fold_in(key, 7)
    subkeys = jax.random.split(folded, 3)
    row_ids = jnp.arange(ROWS, dtype=jnp.int32)
    order = jax.random.permutation(subkeys[0], ROWS).astype(jnp.int32)
    short_row = order[0]
    long_row = order[1]
    audio_count = jax.random.randint(subkeys[1], (ROWS,), LEN // 8, LEN // 2 + 1)
    audio_count = jnp.where(row_ids == short_row, LEN // 2, audio_count)
    audio_count = jnp.where(row_ids == long_row, LEN // 8, audio_count)
    pad_count = jax.random.randint(subkeys[2], (ROWS,), 0, LEN // 4 + 1)
    pad_count = jnp.where(row_ids == short_row, LEN // 4, pad_count)
    pad_count = jnp.where(row_ids == long_row, 0, pad_count)
    return (audio_count.astype(jnp.int32), (LEN - audio_count - pad_count).astype(jnp.int32))


def draw_audio_len(key, part):
    return length_pair(key)[0]


def draw_text_len(key, part):
    return length_pair(key)[1]


def levels(own_key, dims, cuts, least, high):
    def one(axis_at, blocks):
        steps = jax.random.uniform(jax.random.fold_in(jax.random.fold_in(own_key, 6), axis_at), (blocks,), jnp.float32, least / len(cuts), high / len(cuts))
        return jnp.repeat(jnp.exp(steps), dims[axis_at] // blocks).reshape((-1,) + (1,) * (len(dims) - axis_at - 1))

    gain = one(*cuts[0])
    for cut in cuts[1:]:
        gain = gain * one(*cut)
    return gain


def normal_values(stream_key, extent, scale, limit, cuts=(), kind=jnp.bfloat16):
    drawn = scale * jax.random.normal(stream_key, extent, jnp.float32)
    if cuts:
        drawn = drawn * levels(stream_key, extent, cuts, -0.22, 0.18)
    return jnp.clip(drawn, -limit, limit).astype(kind)


def setup_inputs(seed: int = 0) -> dict:
    splits = jax.random.split(jax.random.key(seed), 9)
    frames = normal_values(splits[0], (ROWS, 4 * LEN, FEAT), 1.0, 6.0, ((0, 4), (2, 2)))
    adapter_weight = normal_values(splits[1], (4, FEAT, D), (4 * FEAT) ** -0.5, 0.078125, ((1, 2), (2, 4)))
    text_embed = normal_values(splits[2], (TOKENS, D), 1.0, 6.0, ((0, 4), (1, 4)))
    audio_len = draw_audio_len(jax.random.fold_in(splits[8], 71), 0)
    text_len = draw_text_len(jax.random.fold_in(splits[8], 71), 0)
    norm_gain = jnp.clip(1.0 + 0.1 * jax.random.normal(splits[5], (D,), jnp.float32), 0.5, 1.5).astype(jnp.bfloat16)
    gate_up = normal_values(splits[6], (D, 2, FF), D ** -0.5, 0.046875, ((0, 4), (2, 8)))
    cotangent = normal_values(splits[7], (TOKENS, FF), 0.1, 0.59765625, ((0, 4), (1, 8)))
    return {"frames": frames, "adapter_weight": adapter_weight, "text_embed": text_embed, "audio_len": audio_len, "text_len": text_len, "norm_gain": norm_gain, "gate_up": gate_up, "cotangent": cotangent}


norm_eps = 1e-05

def reference(frames, adapter_weight, text_embed, audio_len, text_len, norm_gain, gate_up, cotangent):
    stacked = frames.reshape(TOKENS, 4 * FEAT)
    kernel = adapter_weight.reshape(4 * FEAT, D)
    audio_part = jnp.dot(stacked, kernel, preferred_element_type=jnp.float32)
    token_ids = jnp.arange(TOKENS, dtype=jnp.int32)
    positions = token_ids % LEN
    row_index = token_ids // LEN
    audio_count = audio_len[row_index]
    text_count = text_len[row_index]
    is_audio = positions < audio_count
    is_text = jnp.logical_and(jnp.logical_not(is_audio), positions < audio_count + text_count)
    stream = jnp.where(is_audio[:, None], audio_part, jnp.where(is_text[:, None], text_embed.astype(jnp.float32), jnp.zeros_like(audio_part)))
    sum_squares = lax.optimization_barrier(jnp.sum(stream * stream, axis=1))
    inv_rms = lax.rsqrt(sum_squares / D + norm_eps)
    unit_stream = stream * inv_rms[:, None]
    gain_vals = norm_gain.astype(jnp.float32)
    normed = (unit_stream * gain_vals[None, :]).astype(jnp.bfloat16)
    weights = gate_up.reshape(D, 2 * FF)
    summed = jnp.dot(normed, weights, preferred_element_type=jnp.float32)
    gate_vals = summed[:, :FF]
    up_vals = summed[:, FF:]
    sigmoid_gate = jax.nn.sigmoid(gate_vals)
    silu_gate = gate_vals * sigmoid_gate
    hidden = (silu_gate * up_vals).astype(jnp.bfloat16)
    cot_vals = cotangent.astype(jnp.float32)
    silu_slope = sigmoid_gate * (1.0 + gate_vals * (1.0 - sigmoid_gate))
    grad_gate = (cot_vals * up_vals * silu_slope).astype(jnp.bfloat16)
    grad_up = (cot_vals * silu_gate).astype(jnp.bfloat16)
    grad_pair = jnp.concatenate([grad_gate, grad_up], axis=1)
    normed_grad = lax.dot_general(grad_pair, weights, (((1,), (1,)), ((), ())), preferred_element_type=jnp.float32)
    scaled_grad = normed_grad * gain_vals[None, :]
    proj_stat = lax.optimization_barrier(jnp.sum(unit_stream * scaled_grad, axis=1)) / D
    stream_grad = (scaled_grad - unit_stream * proj_stat[:, None]) * inv_rms[:, None]
    audio_grad = jnp.where(is_audio[:, None], stream_grad, jnp.zeros_like(stream_grad)).astype(jnp.bfloat16)
    weight_grad = lax.dot_general(stacked, audio_grad, (((0,), (0,)), ((), ())), preferred_element_type=jnp.float32)
    return (hidden, weight_grad.reshape(4, FEAT, D))
```

```python
import jax
import jax.numpy as jnp
from jax import lax
from jax.experimental import pallas as pl
from jax.experimental.pallas import tpu as pltpu
from jax.sharding import PartitionSpec as P


norm_eps = 1e-05
bf16, f16, f32 = jnp.bfloat16, jnp.float16, jnp.float32
audio_scale = 16.0
gate_scale = 32.0


def tied(value, *after):
    return lax.optimization_barrier((value,) + after)[0]


def bits(count):
    steps, step = [], 1
    while step < count:
        steps.append(step)
        step *= 2
    return steps


def swap(value, axis, step):
    return lax.ppermute(value, axis, [(i, i ^ step) for i in range(lax.axis_size(axis))])


def bit_of(axis, step):
    return (lax.axis_index(axis) // step) % 2


def put_pair(own, got, bit, dim):
    at = dim + 1
    shape = own.shape[:at] + (2,) + own.shape[at:]
    out = jnp.zeros(shape, own.dtype)
    out = lax.dynamic_update_slice_in_dim(out, jnp.expand_dims(own, at), bit, at)
    out = lax.dynamic_update_slice_in_dim(out, jnp.expand_dims(got, at), 1 - bit, at)
    return out.reshape(own.shape[:dim] + (-1,) + own.shape[at:])


def join(value, axis, step, dim):
    return put_pair(value, swap(value, axis, step), bit_of(axis, step), dim)


def spread(value, axis):
    out = value[None]
    for step in bits(lax.axis_size(axis))[::-1]:
        out = join(out, axis, step, 0)
    return out


def halve(value, axis, step, dim):
    bit = bit_of(axis, step)
    shape = value.shape
    pairs = value.reshape(shape[:dim] + (shape[dim] // 2, 2) + shape[dim + 1 :])
    kept = lax.dynamic_index_in_dim(pairs, bit, dim + 1, keepdims=False)
    sent = lax.dynamic_index_in_dim(pairs, 1 - bit, dim + 1, keepdims=False).astype(bf16)
    return kept + swap(sent, axis, step).astype(f32)


def quad_swap(value, axes, flips):
    sizes = [lax.axis_size(a) for a in axes]
    tops = [(n // 2) * f for n, f in zip(sizes, flips)]
    pairs = [
        (i * sizes[1] + j, (i ^ tops[0]) * sizes[1] + (j ^ tops[1]))
        for i in range(sizes[0])
        for j in range(sizes[1])
    ]
    return lax.ppermute(value, axes, pairs)


flips_of_quad = ((1, 0), (0, 1), (1, 1))


def top_bits(axes):
    return [bit_of(a, lax.axis_size(a) // 2) for a in axes]


def quad_sum(value, axes):
    x, y = top_bits(axes)

    def block(i, j):
        out = lax.dynamic_index_in_dim(value, i, 0, keepdims=False)
        return lax.dynamic_index_in_dim(out, j, 0, keepdims=False)

    total = block(x, y)
    for fx, fy in flips_of_quad:
        sent = block(x ^ fx, y ^ fy).astype(bf16)
        total = total + quad_swap(sent, axes, (fx, fy)).astype(f32)
    return total


def quad_spread(value, axes):
    x, y = top_bits(axes)
    out = jnp.zeros((2, 2) + value.shape, value.dtype)
    out = lax.dynamic_update_slice(out, value[None, None], (x, y, 0, 0))
    for fx, fy in flips_of_quad:
        got = quad_swap(value, axes, (fx, fy))
        out = lax.dynamic_update_slice(out, got[None, None], (x ^ fx, y ^ fy, 0, 0))
    return out


def line_sum(value, axis):
    n = lax.axis_size(axis)
    total = value
    for shift in range(1, n):
        total = total + lax.ppermute(value, axis, [(i, (i + shift) % n) for i in range(n)])
    return total


def right_of(n, tick, gather):
    return [(i, i + 1) for i in range(n - 1) if (i >= tick - 1 if gather else i < tick)]


def left_of(n, tick, gather):
    return [(n - 1 - i, n - 1 - j) for i, j in right_of(n, tick, gather)]


def line_scatter(parts, axis):
    n = lax.axis_size(axis)
    z = lax.axis_index(axis)

    def block(s):
        s = jnp.clip(s, 0, n - 1)
        blocks = [lax.dynamic_index_in_dim(p, s, 0, keepdims=False) for p in parts]
        return jnp.concatenate(blocks, axis=-1)

    right = left = None
    for tick in range(1, n):
        to_right, to_left = block(n + z - tick), block(z + tick - n)
        if tick > 1:
            to_right, to_left = to_right + right, to_left + left
        right = (to_right * gate_scale).astype(f16)
        left = (to_left * gate_scale).astype(f16)
        right = lax.ppermute(right, axis, right_of(n, tick, False))
        left = lax.ppermute(left, axis, left_of(n, tick, False))
        right, left = (v.astype(f32) * (1.0 / gate_scale) for v in (right, left))
    return block(z) + right + left


def back_kernel(grads_ref, gate_ref, up_ref, *refs):
    span = gate_ref.shape[1]
    dims = (((1,), (1,)), ((), ()))
    total = lax.dot_general(
        grads_ref[:, :span], gate_ref[...], dims, preferred_element_type=f32
    ) + lax.dot_general(grads_ref[:, span:], up_ref[...], dims, preferred_element_type=f32)
    if len(refs) == 2:
        total = total + refs[0][...]
    refs[-1][...] = total


def back(grads, w, c, chunks, so_far):
    rows, span = grads.shape[0], grads.shape[1] // 2
    width = w.shape[0]
    if span % 128:
        cols = jnp.concatenate(
            [w[:, (k * chunks + c) * span : (k * chunks + c + 1) * span] for k in range(2)], axis=1
        )
        total = lax.dot_general(
            grads, cols, (((1,), (1,)), ((), ())), preferred_element_type=f32
        )
        return total if so_far is None else total + so_far
    block = 512
    while width % block:
        block //= 2
    out_spec = pl.BlockSpec((rows, block), lambda i: (0, i))
    in_specs = [
        pl.BlockSpec((rows, 2 * span), lambda i: (0, 0)),
        pl.BlockSpec((block, span), lambda i: (i, c)),
        pl.BlockSpec((block, span), lambda i: (i, chunks + c)),
    ]
    args = [grads, w, w]
    if so_far is not None:
        in_specs.append(out_spec)
        args.append(so_far)
    return pl.pallas_call(
        back_kernel,
        grid=(width // block,),
        in_specs=in_specs,
        out_specs=out_spec,
        out_shape=jax.ShapeDtypeStruct((rows, width), f32),
        input_output_aliases={3: 0} if so_far is not None else {},
        compiler_params=pltpu.CompilerParams(vmem_limit_bytes=48 * 2**20),
        cost_estimate=pl.CostEstimate(
            flops=4 * rows * span * width,
            bytes_accessed=4 * width * span + 4 * rows * span + 4 * rows * width,
            transcendentals=0,
        ),
    )(*args)


def on_device(
    frames, adapter_weight, text_embed, audio_len, text_len, norm_gain, gate_up, cotangent
):
    frame_count, feat_here = frames.shape[1:]
    seq_len = frame_count // 4
    cap = seq_len // 2
    width_here = adapter_weight.shape[2]
    full_width = width_here * lax.axis_size("width")
    units = gate_up.shape[2]
    gain = norm_gain.astype(f32)[None, :]

    chunks = 2 if units % 256 == 0 else 1
    span = units // chunks

    places = jnp.arange(seq_len, dtype=jnp.int32)
    is_audio = (places[:cap] < audio_len[0])[:, None]
    is_text = (places < audio_len[0] + text_len[0])[:, None]
    text_rows = jnp.where(is_text, text_embed.astype(f32), 0.0)

    def inverse(squares):
        total = line_sum(squares, "width")
        return lax.rsqrt(total / full_width + norm_eps)[:, None]

    tail = text_rows[cap:]
    tail_squares = jnp.sum(tail * tail, axis=1)
    tail_norm = (tail * inverse(tail_squares) * gain).astype(bf16)
    tail_rows = spread(tail_norm, "batch")

    stacked = frames[0, : 4 * cap].reshape(cap, 4 * feat_here)
    kernel = adapter_weight.reshape(4 * feat_here, width_here)
    half = width_here // 2
    pieces = []
    for lo in (0, half):
        audio = jnp.dot(tied(stacked, tail_squares), kernel[:, lo : lo + half], preferred_element_type=f32)
        for step in bits(lax.axis_size("hidden")):
            got = swap((audio * audio_scale).astype(f16), "hidden", step)
            audio = audio + got.astype(f32) * (1.0 / audio_scale)
        pieces.append(audio)
    audio = jnp.concatenate(pieces, axis=1)
    head = jnp.where(is_audio, audio, text_rows[:cap])
    inv_rms = inverse(jnp.sum(head * head, axis=1))
    unit = head * inv_rms
    head_rows = spread((unit * gain).astype(bf16), "batch")
    count = head_rows.shape[0]
    n_head = count * cap

    rows = jnp.concatenate([head_rows, tail_rows], axis=0).reshape(2 * n_head, width_here)
    part = jnp.einsum("tf,fgh->gth", rows, gate_up, preferred_element_type=f32)
    part = lax.optimization_barrier(part)
    stack_all = spread(tied(stacked, part), "batch").reshape(n_head, 4 * feat_here)

    def chunk(c):
        return [part[k, :n_head, c * span : (c + 1) * span] for k in range(2)]

    def gates(summed):
        gate, up = jnp.split(summed, 2, axis=1)
        sig = jax.nn.sigmoid(gate)
        return gate, up, sig, gate * sig

    hidden_head, pairs, proj = [], [], 0.0
    for c in range(chunks):
        got = line_scatter([p.reshape(count, cap, span) for p in chunk(c)], "width")
        gate, up, sig, silu = gates(got)
        hidden_head.append((silu * up).astype(bf16))
        cot = cotangent[:cap, c * span : (c + 1) * span].astype(f32)
        slope = sig * (1.0 + gate * (1.0 - sig))
        grads = [(cot * up * slope).astype(bf16), (cot * silu).astype(bf16)]
        proj = proj + jnp.sum(gate * grads[0].astype(f32) + up * grads[1].astype(f32), axis=1)
        grads = jnp.concatenate(grads, axis=1)
        pairs.append(lax.all_gather(grads, "width", axis=0, tiled=True))

    last = pairs[-1]
    w = lax.optimization_barrier(tied(gate_up, grads).reshape(width_here, 2 * units))
    rest = lax.optimization_barrier((part[0, n_head:], part[1, n_head:], grads))[:2]
    rest = jnp.concatenate([p.astype(bf16) for p in rest], axis=1)
    proj = tied(proj, grads)

    lines = lax.axis_size("width")
    z = lax.axis_index("width")
    shared = jnp.zeros((lines, cap), f32)
    shared = lax.dynamic_update_slice_in_dim(shared, proj[None], z, 0)
    for shift in range(1, lines):
        ring = [(i, (i + shift) % lines) for i in range(lines)]
        got = lax.ppermute(proj, "width", ring)
        shared = lax.dynamic_update_slice_in_dim(shared, got[None], (z - shift) % lines, 0)
    for axis in ("batch", "hidden"):
        for step in bits(lax.axis_size(axis)):
            shared = shared + swap(shared, axis, step)

    pairs[-1], shared, rest = lax.optimization_barrier((pairs[-1], shared, rest))
    grad = None
    for c in range(chunks):
        grad = back(pairs[c], w, c, chunks, grad)

    groups = lax.axis_size("hidden")
    share = cap // groups
    grad = grad.reshape(count, groups, share, width_here)
    low = [("batch", step, 0) for step in bits(lax.axis_size("batch"))[:-1]]
    low += [("hidden", step, 1) for step in bits(groups)[:-1]]
    quad = ("batch", "hidden")
    for step in low:
        grad = halve(grad, *step)
    scaled = quad_sum(grad, quad) * gain
    start = lax.axis_index("hidden") * share
    unit = lax.dynamic_slice_in_dim(unit, start, share, 0)
    inv = lax.dynamic_slice_in_dim(inv_rms, start, share, 0)
    own = lax.axis_index("batch")
    proj = lax.dynamic_slice(shared, (own, start), (1, share))[0][:, None] / full_width
    grad = (scaled - unit * proj) * inv
    mine = (start + jnp.arange(share, dtype=jnp.int32) < audio_len[0])[:, None]
    grad = quad_spread(jnp.where(mine, grad, 0.0).astype(bf16), quad)
    for step in low[::-1]:
        grad = join(grad, *step)
    weight_grad = lax.dot_general(
        stack_all,
        grad.reshape(n_head, width_here),
        (((0,), (0,)), ((), ())),
        preferred_element_type=f32,
    )

    rest = lax.psum_scatter(tied(rest, last), "width", scatter_dimension=0, tiled=True)
    rest, weight_grad = lax.optimization_barrier((rest, weight_grad))
    _, up, _, silu = gates(rest.astype(f32))
    hidden_tail = (silu * up).astype(bf16)
    hidden = jnp.concatenate([jnp.concatenate(hidden_head, axis=1), hidden_tail], axis=0)
    return (hidden, weight_grad.reshape(4, feat_here, width_here))


def solution(mesh):
    return jax.shard_map(
        on_device,
        mesh=mesh,
        in_specs=(
            P("batch", None, "hidden"),
            P(None, "hidden", "width"),
            P("batch", "width"),
            P("batch"),
            P("batch"),
            P("width"),
            P("width", None, ("batch", "hidden")),
            P("width", ("batch", "hidden")),
        ),
        out_specs=(P("width", ("batch", "hidden")), P(None, "hidden", "width")),
        check_vma=False,
    )
```

```python
import jax
import jax.numpy as jnp
from jax import lax
from jax.experimental import pallas as pl
from jax.experimental.pallas import tpu as pltpu
from jax.sharding import PartitionSpec as P


norm_eps = 1e-05
bf16, f16, f32 = jnp.bfloat16, jnp.float16, jnp.float32
audio_scale = 16.0
gate_scale = 32.0


def tied(value, *after):
    return lax.optimization_barrier((value,) + after)[0]


def bits(count):
    steps, step = [], 1
    while step < count:
        steps.append(step)
        step *= 2
    return steps


def swap(value, axis, step):
    return lax.ppermute(value, axis, [(i, i ^ step) for i in range(lax.axis_size(axis))])


def bit_of(axis, step):
    return (lax.axis_index(axis) // step) % 2


def put_pair(own, got, bit, dim):
    at = dim + 1
    shape = own.shape[:at] + (2,) + own.shape[at:]
    out = jnp.zeros(shape, own.dtype)
    out = lax.dynamic_update_slice_in_dim(out, jnp.expand_dims(own, at), bit, at)
    out = lax.dynamic_update_slice_in_dim(out, jnp.expand_dims(got, at), 1 - bit, at)
    return out.reshape(own.shape[:dim] + (-1,) + own.shape[at:])


def join(value, axis, step, dim):
    return put_pair(value, swap(value, axis, step), bit_of(axis, step), dim)


def spread(value, axis):
    out = value[None]
    for step in bits(lax.axis_size(axis))[::-1]:
        out = join(out, axis, step, 0)
    return out


def direct(value, axis):
    n = lax.axis_size(axis)
    index = lax.axis_index(axis)
    out = jnp.zeros((n,) + value.shape, value.dtype)
    out = lax.dynamic_update_slice_in_dim(out, value[None], index, 0)
    for step in range(1, n):
        got = swap(value, axis, step)[None]
        out = lax.dynamic_update_slice_in_dim(out, got, index ^ step, 0)
    return out


def halve(value, axis, step, dim):
    bit = bit_of(axis, step)
    shape = value.shape
    pairs = value.reshape(shape[:dim] + (shape[dim] // 2, 2) + shape[dim + 1 :])
    kept = lax.dynamic_index_in_dim(pairs, bit, dim + 1, keepdims=False)
    sent = lax.dynamic_index_in_dim(pairs, 1 - bit, dim + 1, keepdims=False).astype(bf16)
    return kept + swap(sent, axis, step).astype(f32)


def quad_swap(value, axes, flips):
    sizes = [lax.axis_size(a) for a in axes]
    tops = [(n // 2) * f for n, f in zip(sizes, flips)]
    pairs = [
        (i * sizes[1] + j, (i ^ tops[0]) * sizes[1] + (j ^ tops[1]))
        for i in range(sizes[0])
        for j in range(sizes[1])
    ]
    return lax.ppermute(value, axes, pairs)


flips_of_quad = ((1, 0), (0, 1), (1, 1))


def top_bits(axes):
    return [bit_of(a, lax.axis_size(a) // 2) for a in axes]


def quad_sum(value, axes):
    x, y = top_bits(axes)

    def block(i, j):
        out = lax.dynamic_index_in_dim(value, i, 0, keepdims=False)
        return lax.dynamic_index_in_dim(out, j, 0, keepdims=False)

    total = block(x, y)
    for fx, fy in flips_of_quad:
        sent = block(x ^ fx, y ^ fy).astype(bf16)
        total = total + quad_swap(sent, axes, (fx, fy)).astype(f32)
    return total


def quad_spread(value, axes):
    x, y = top_bits(axes)
    out = jnp.zeros((2, 2) + value.shape, value.dtype)
    out = lax.dynamic_update_slice(out, value[None, None], (x, y, 0, 0))
    for fx, fy in flips_of_quad:
        got = quad_swap(value, axes, (fx, fy))
        out = lax.dynamic_update_slice(out, got[None, None], (x ^ fx, y ^ fy, 0, 0))
    return out


def line_sum(value, axis):
    n = lax.axis_size(axis)
    total = value
    for shift in range(1, n):
        total = total + lax.ppermute(value, axis, [(i, (i + shift) % n) for i in range(n)])
    return total


def right_of(n, tick, gather):
    return [(i, i + 1) for i in range(n - 1) if (i >= tick - 1 if gather else i < tick)]


def left_of(n, tick, gather):
    return [(n - 1 - i, n - 1 - j) for i, j in right_of(n, tick, gather)]


def line_scatter(part, lo, span, rows, axis):
    n = lax.axis_size(axis)
    z = lax.axis_index(axis)

    def block(source, s):
        at = jnp.clip(s, 0, n - 1) * rows
        blocks = [lax.dynamic_slice(source, (k, at, lo), (1, rows, span))[0] for k in range(2)]
        return jnp.concatenate(blocks, axis=-1)

    right = left = None
    for tick in range(1, n):
        source = part if tick == 1 else tied(part, right)
        to_right, to_left = block(source, n + z - tick), block(source, z + tick - n)
        if tick > 1:
            to_right, to_left = to_right + right, to_left + left
        right = (to_right * gate_scale).astype(f16)
        left = (to_left * gate_scale).astype(f16)
        right = lax.ppermute(right, axis, right_of(n, tick, False))
        left = lax.ppermute(left, axis, left_of(n, tick, False))
        right, left = (v.astype(f32) * (1.0 / gate_scale) for v in (right, left))
    return block(tied(part, right), z) + right + left


def back_kernel(grads_ref, gate_ref, up_ref, *refs):
    span = gate_ref.shape[1]
    dims = (((1,), (1,)), ((), ()))
    total = lax.dot_general(
        grads_ref[:, :span], gate_ref[...], dims, preferred_element_type=f32
    ) + lax.dot_general(grads_ref[:, span:], up_ref[...], dims, preferred_element_type=f32)
    if len(refs) == 2:
        total = total + refs[0][...]
    refs[-1][...] = total


def back(grads, w, c, chunks, so_far):
    rows, span = grads.shape[0], grads.shape[1] // 2
    width = w.shape[0]
    if span % 128:
        cols = jnp.concatenate(
            [w[:, (k * chunks + c) * span : (k * chunks + c + 1) * span] for k in range(2)], axis=1
        )
        total = lax.dot_general(
            grads, cols, (((1,), (1,)), ((), ())), preferred_element_type=f32
        )
        return total if so_far is None else total + so_far
    block = 512
    while width % block:
        block //= 2
    out_spec = pl.BlockSpec((rows, block), lambda i: (0, i))
    in_specs = [
        pl.BlockSpec((rows, 2 * span), lambda i: (0, 0)),
        pl.BlockSpec((block, span), lambda i: (i, c)),
        pl.BlockSpec((block, span), lambda i: (i, chunks + c)),
    ]
    args = [grads, w, w]
    if so_far is not None:
        in_specs.append(out_spec)
        args.append(so_far)
    return pl.pallas_call(
        back_kernel,
        grid=(width // block,),
        in_specs=in_specs,
        out_specs=out_spec,
        out_shape=jax.ShapeDtypeStruct((rows, width), f32),
        input_output_aliases={3: 0} if so_far is not None else {},
        compiler_params=pltpu.CompilerParams(vmem_limit_bytes=60 * 1024 * 2**10),
        cost_estimate=pl.CostEstimate(
            flops=4 * rows * span * width,
            bytes_accessed=4 * width * span + 4 * rows * span + 4 * rows * width,
            transcendentals=0,
        ),
    )(*args)


def on_device(
    frames, adapter_weight, text_embed, audio_len, text_len, norm_gain, gate_up, cotangent
):
    frame_count, feat_here = frames.shape[1:]
    seq_len = frame_count // 4
    cap = seq_len // 2
    width_here = adapter_weight.shape[2]
    full_width = width_here * lax.axis_size("width")
    units = gate_up.shape[2]
    gain = norm_gain.astype(f32)[None, :]

    chunks = 2 if units % 256 == 0 else 1
    span = units // chunks

    places = jnp.arange(seq_len, dtype=jnp.int32)
    is_audio = (places[:cap] < audio_len[0])[:, None]
    is_text = (places < audio_len[0] + text_len[0])[:, None]
    text_rows = jnp.where(is_text, text_embed.astype(f32), 0.0)

    tail_all = spread(jnp.where(is_text[cap:], text_embed[cap:], 0), "batch")

    stacked = frames[0, : 4 * cap].reshape(cap, 4 * feat_here)
    kernel = adapter_weight.reshape(4 * feat_here, width_here)
    half = width_here // 2
    pieces = []
    for lo in (0, half):
        for step in bits(lax.axis_size("hidden")):
            if step == 1:
                audio = jnp.dot(
                    stacked, kernel[:, lo : lo + half], preferred_element_type=f32
                )
            sent = (audio * audio_scale).astype(f16)
            got = swap(sent, "hidden", step)
            audio = audio + got.astype(f32) * (1.0 / audio_scale)
        pieces.append(audio)
    audio = jnp.concatenate(pieces, axis=1)
    head = jnp.where(is_audio, audio, text_rows[:cap])
    head_all = spread((head * audio_scale).astype(f16), "batch")
    count = head_all.shape[0]
    n_head = count * cap
    tail = text_rows[cap:]
    squares = jnp.concatenate([jnp.sum(head * head, axis=1), jnp.sum(tail * tail, axis=1)])
    inv_own = lax.rsqrt(line_sum(squares, "width") / full_width + norm_eps)
    inv_all = direct(inv_own, "batch")
    inv_rms = inv_own[:, None]
    unit = head * inv_rms[:cap]
    rows = jnp.stack([head_all.astype(f32) * (1.0 / audio_scale), tail_all.astype(f32)])
    scales = jnp.stack([inv_all[:, :cap], inv_all[:, cap:]])[..., None]
    rows = (rows * scales * gain).astype(bf16).reshape(2 * n_head, width_here)
    part = jnp.einsum("tf,fgh->gth", rows, gate_up, preferred_element_type=f32)
    part = lax.optimization_barrier(part)
    stack_all = spread(tied(stacked, part), "batch").reshape(n_head, 4 * feat_here)

    def gates(summed):
        gate, up = jnp.split(summed, 2, axis=1)
        sig = jax.nn.sigmoid(gate)
        return gate, up, sig, gate * sig

    rest = lax.optimization_barrier((part[0, n_head:], part[1, n_head:]))
    rest = jnp.concatenate([p.astype(bf16) for p in rest], axis=1)
    hidden_head, pairs, proj = [], [], 0.0
    for c in range(chunks):
        got = line_scatter(part, c * span, span, cap, "width")
        if c == 0:
            got, stack_all, rest = lax.optimization_barrier((got, stack_all, rest))
        if c:
            got = tied(got, grads)
        gate, up, sig, silu = gates(got)
        hidden_head.append((silu * up).astype(bf16))
        cot = cotangent[:cap, c * span : (c + 1) * span].astype(f32)
        slope = sig * (1.0 + gate * (1.0 - sig))
        grads = [(cot * up * slope).astype(bf16), (cot * silu).astype(bf16)]
        proj = proj + jnp.sum(gate * grads[0].astype(f32) + up * grads[1].astype(f32), axis=1)
        grads = jnp.concatenate(grads, axis=1)
        pairs.append(lax.all_gather(grads, "width", axis=0, tiled=True))

    last = pairs[-1]
    w = lax.optimization_barrier(tied(gate_up, grads).reshape(width_here, 2 * units))
    proj = tied(proj, grads)

    lines = lax.axis_size("width")
    z = lax.axis_index("width")
    shared = jnp.zeros((lines, cap), f32)
    shared = lax.dynamic_update_slice_in_dim(shared, proj[None], z, 0)
    for shift in range(1, lines):
        ring = [(i, (i + shift) % lines) for i in range(lines)]
        got = lax.ppermute(proj, "width", ring)
        shared = lax.dynamic_update_slice_in_dim(shared, got[None], (z - shift) % lines, 0)
    for axis in ("batch", "hidden"):
        for step in bits(lax.axis_size(axis)):
            shared = shared + swap(shared, axis, step)

    pairs[0], shared = lax.optimization_barrier((pairs[0], shared))
    grad = None
    for c in range(chunks):
        grad = back(pairs[c], w, c, chunks, grad)

    groups = lax.axis_size("hidden")
    share = cap // groups
    grad = grad.reshape(count, groups, share, width_here)
    low = [("batch", step, 0) for step in bits(lax.axis_size("batch"))[:-1]]
    low += [("hidden", step, 1) for step in bits(groups)[:-1]]
    quad = ("batch", "hidden")
    for step in low:
        grad = halve(grad, *step)
    scaled = quad_sum(grad, quad) * gain
    start = lax.axis_index("hidden") * share
    unit = lax.dynamic_slice_in_dim(unit, start, share, 0)
    inv = lax.dynamic_slice_in_dim(inv_rms, start, share, 0)
    own = lax.axis_index("batch")
    proj = lax.dynamic_slice(shared, (own, start), (1, share))[0][:, None] / full_width
    grad = (scaled - unit * proj) * inv
    mine = (start + jnp.arange(share, dtype=jnp.int32) < audio_len[0])[:, None]
    grad = quad_spread(jnp.where(mine, grad, 0.0).astype(bf16), quad)
    for step in low[::-1]:
        grad = join(grad, *step)
    weight_grad = lax.dot_general(
        stack_all,
        grad.reshape(n_head, width_here),
        (((0,), (0,)), ((), ())),
        preferred_element_type=f32,
    )

    rest = lax.psum_scatter(tied(rest, last), "width", scatter_dimension=0, tiled=True)
    rest, weight_grad = lax.optimization_barrier((rest, weight_grad))
    _, up, _, silu = gates(rest.astype(f32))
    hidden_tail = (silu * up).astype(bf16)
    hidden = jnp.concatenate([jnp.concatenate(hidden_head, axis=1), hidden_tail], axis=0)
    return (hidden, weight_grad.reshape(4, feat_here, width_here))


def solution(mesh):
    return jax.shard_map(
        on_device,
        mesh=mesh,
        in_specs=(
            P("batch", None, "hidden"),
            P(None, "hidden", "width"),
            P("batch", "width"),
            P("batch"),
            P("batch"),
            P("width"),
            P("width", None, ("batch", "hidden")),
            P("width", ("batch", "hidden")),
        ),
        out_specs=(P("width", ("batch", "hidden")), P(None, "hidden", "width")),
        check_vma=False,
    )
```

```python
import jax
import jax.numpy as jnp
from jax import lax
from jax.experimental import pallas as pl
from jax.experimental.pallas import tpu as pltpu
from jax.sharding import PartitionSpec as P


norm_eps = 1e-05
bf16, f16, f32 = jnp.bfloat16, jnp.float16, jnp.float32
audio_scale = 16.0
gate_scale = 32.0


def tied(value, *after):
    return lax.optimization_barrier((value,) + after)[0]


def bits(count):
    steps, step = [], 1
    while step < count:
        steps.append(step)
        step *= 2
    return steps


def swap(value, axis, step):
    return lax.ppermute(value, axis, [(i, i ^ step) for i in range(lax.axis_size(axis))])


def bit_of(axis, step):
    return (lax.axis_index(axis) // step) % 2


def put_pair(own, got, bit, dim):
    at = dim + 1
    shape = own.shape[:at] + (2,) + own.shape[at:]
    out = jnp.zeros(shape, own.dtype)
    out = lax.dynamic_update_slice_in_dim(out, jnp.expand_dims(own, at), bit, at)
    out = lax.dynamic_update_slice_in_dim(out, jnp.expand_dims(got, at), 1 - bit, at)
    return out.reshape(own.shape[:dim] + (-1,) + own.shape[at:])


def join(value, axis, step, dim):
    return put_pair(value, swap(value, axis, step), bit_of(axis, step), dim)


def spread(value, axis):
    out = value[None]
    for step in bits(lax.axis_size(axis))[::-1]:
        out = join(out, axis, step, 0)
    return out


def direct(value, axis):
    n = lax.axis_size(axis)
    index = lax.axis_index(axis)
    out = jnp.zeros((n,) + value.shape, value.dtype)
    out = lax.dynamic_update_slice_in_dim(out, value[None], index, 0)
    for step in range(1, n):
        got = swap(value, axis, step)[None]
        out = lax.dynamic_update_slice_in_dim(out, got, index ^ step, 0)
    return out


def halve(value, axis, step, dim):
    bit = bit_of(axis, step)
    shape = value.shape
    pairs = value.reshape(shape[:dim] + (shape[dim] // 2, 2) + shape[dim + 1 :])
    kept = lax.dynamic_index_in_dim(pairs, bit, dim + 1, keepdims=False)
    sent = lax.dynamic_index_in_dim(pairs, 1 - bit, dim + 1, keepdims=False).astype(bf16)
    return kept + swap(sent, axis, step).astype(f32)


def quad_swap(value, axes, flips):
    sizes = [lax.axis_size(a) for a in axes]
    tops = [(n // 2) * f for n, f in zip(sizes, flips)]
    pairs = [
        (i * sizes[1] + j, (i ^ tops[0]) * sizes[1] + (j ^ tops[1]))
        for i in range(sizes[0])
        for j in range(sizes[1])
    ]
    return lax.ppermute(value, axes, pairs)


flips_of_quad = ((1, 0), (0, 1), (1, 1))


def top_bits(axes):
    return [bit_of(a, lax.axis_size(a) // 2) for a in axes]


def quad_sum(value, axes):
    x, y = top_bits(axes)

    def block(i, j):
        out = lax.dynamic_index_in_dim(value, i, 0, keepdims=False)
        return lax.dynamic_index_in_dim(out, j, 0, keepdims=False)

    total = block(x, y)
    for fx, fy in flips_of_quad:
        sent = block(x ^ fx, y ^ fy).astype(bf16)
        total = total + quad_swap(sent, axes, (fx, fy)).astype(f32)
    return total


def quad_spread(value, axes):
    x, y = top_bits(axes)
    out = jnp.zeros((2, 2) + value.shape, value.dtype)
    out = lax.dynamic_update_slice(out, value[None, None], (x, y, 0, 0))
    for fx, fy in flips_of_quad:
        got = quad_swap(value, axes, (fx, fy))
        out = lax.dynamic_update_slice(out, got[None, None], (x ^ fx, y ^ fy, 0, 0))
    return out


def line_sum(value, axis):
    n = lax.axis_size(axis)
    total = value
    for shift in range(1, n):
        total = total + lax.ppermute(value, axis, [(i, (i + shift) % n) for i in range(n)])
    return total


def right_of(n, tick, gather):
    return [(i, i + 1) for i in range(n - 1) if (i >= tick - 1 if gather else i < tick)]


def left_of(n, tick, gather):
    return [(n - 1 - i, n - 1 - j) for i, j in right_of(n, tick, gather)]


def line_scatter(part, lo, span, rows, axis):
    n = lax.axis_size(axis)
    z = lax.axis_index(axis)

    def block(source, s):
        at = jnp.clip(s, 0, n - 1) * rows
        blocks = [lax.dynamic_slice(source, (k, at, lo), (1, rows, span))[0] for k in range(2)]
        return jnp.concatenate(blocks, axis=-1)

    right = left = None
    for tick in range(1, n):
        source = part if tick == 1 else tied(part, right)
        to_right, to_left = block(source, n + z - tick), block(source, z + tick - n)
        if tick > 1:
            to_right, to_left = to_right + right, to_left + left
        right = (to_right * gate_scale).astype(f16)
        left = (to_left * gate_scale).astype(f16)
        right = lax.ppermute(right, axis, right_of(n, tick, False))
        left = lax.ppermute(left, axis, left_of(n, tick, False))
        right, left = (v.astype(f32) * (1.0 / gate_scale) for v in (right, left))
    return block(tied(part, right), z) + right + left


def back_kernel(grads_ref, gate_ref, up_ref, *refs):
    span = gate_ref.shape[1]
    dims = (((1,), (1,)), ((), ()))
    total = lax.dot_general(
        grads_ref[:, :span], gate_ref[...], dims, preferred_element_type=f32
    ) + lax.dot_general(grads_ref[:, span:], up_ref[...], dims, preferred_element_type=f32)
    if len(refs) == 2:
        total = total + refs[0][...]
    refs[-1][...] = total


def back(grads, w, c, chunks, so_far):
    rows, span = grads.shape[0], grads.shape[1] // 2
    width = w.shape[0]
    if span % 128:
        cols = jnp.concatenate(
            [w[:, (k * chunks + c) * span : (k * chunks + c + 1) * span] for k in range(2)], axis=1
        )
        total = lax.dot_general(
            grads, cols, (((1,), (1,)), ((), ())), preferred_element_type=f32
        )
        return total if so_far is None else total + so_far
    block = 512
    while width % block:
        block //= 2
    out_spec = pl.BlockSpec((rows, block), lambda i: (0, i))
    in_specs = [
        pl.BlockSpec((rows, 2 * span), lambda i: (0, 0)),
        pl.BlockSpec((block, span), lambda i: (i, c)),
        pl.BlockSpec((block, span), lambda i: (i, chunks + c)),
    ]
    args = [grads, w, w]
    if so_far is not None:
        in_specs.append(out_spec)
        args.append(so_far)
    return pl.pallas_call(
        back_kernel,
        grid=(width // block,),
        in_specs=in_specs,
        out_specs=out_spec,
        out_shape=jax.ShapeDtypeStruct((rows, width), f32),
        input_output_aliases={3: 0} if so_far is not None else {},
        compiler_params=pltpu.CompilerParams(vmem_limit_bytes=60 * 1024 * 2**10),
        cost_estimate=pl.CostEstimate(
            flops=4 * rows * span * width,
            bytes_accessed=4 * width * span + 4 * rows * span + 4 * rows * width,
            transcendentals=0,
        ),
    )(*args)


def on_device(
    frames, adapter_weight, text_embed, audio_len, text_len, norm_gain, gate_up, cotangent
):
    frame_count, feat_here = frames.shape[1:]
    seq_len = frame_count // 4
    cap = seq_len // 2
    width_here = adapter_weight.shape[2]
    full_width = width_here * lax.axis_size("width")
    units = gate_up.shape[2]
    gain = norm_gain.astype(f32)[None, :]

    chunks = 2 if units % 256 == 0 else 1
    span = units // chunks

    places = jnp.arange(seq_len, dtype=jnp.int32)
    is_audio = (places[:cap] < audio_len[0])[:, None]
    is_text = (places < audio_len[0] + text_len[0])[:, None]
    text_rows = jnp.where(is_text, text_embed.astype(f32), 0.0)

    tail_all = spread(jnp.where(is_text[cap:], text_embed[cap:], 0), "batch")

    stacked = frames[0, : 4 * cap].reshape(cap, 4 * feat_here)
    kernel = adapter_weight.reshape(4 * feat_here, width_here)
    half = width_here // 2
    pieces = []
    for lo in (0, half):
        for step in bits(lax.axis_size("hidden")):
            if step == 1:
                audio = jnp.dot(
                    stacked, kernel[:, lo : lo + half], preferred_element_type=f32
                )
            sent = (audio * audio_scale).astype(f16)
            got = swap(sent, "hidden", step)
            audio = audio + got.astype(f32) * (1.0 / audio_scale)
        pieces.append(audio)
    audio = jnp.concatenate(pieces, axis=1)
    head = jnp.where(is_audio, audio, text_rows[:cap])
    head_all = spread((head * audio_scale).astype(f16), "batch")
    count = head_all.shape[0]
    n_head = count * cap
    tail = text_rows[cap:]
    squares = jnp.concatenate([jnp.sum(head * head, axis=1), jnp.sum(tail * tail, axis=1)])
    inv_own = lax.rsqrt(line_sum(squares, "width") / full_width + norm_eps)
    inv_all = direct(inv_own, "batch")
    inv_rms = inv_own[:, None]
    unit = head * inv_rms[:cap]
    rows = jnp.stack([head_all.astype(f32) * (1.0 / audio_scale), tail_all.astype(f32)])
    scales = jnp.stack([inv_all[:, :cap], inv_all[:, cap:]])[..., None]
    rows = (rows * scales * gain).astype(bf16).reshape(2 * n_head, width_here)
    part = jnp.einsum("tf,fgh->gth", rows, gate_up, preferred_element_type=f32)
    part = lax.optimization_barrier(part)
    stack_all = spread(tied(stacked, part), "batch").reshape(n_head, 4 * feat_here)

    def gates(summed):
        gate, up = jnp.split(summed, 2, axis=1)
        sig = jax.nn.sigmoid(gate)
        return gate, up, sig, gate * sig

    hidden_head, pairs, proj = [], [], 0.0
    for c in range(chunks):
        got = line_scatter(part, c * span, span, cap, "width")
        if c == 0:
            got, stack_all = lax.optimization_barrier((got, stack_all))
        if c:
            got = tied(got, grads)
        gate, up, sig, silu = gates(got)
        hidden_head.append((silu * up).astype(bf16))
        cot = cotangent[:cap, c * span : (c + 1) * span].astype(f32)
        slope = sig * (1.0 + gate * (1.0 - sig))
        grads = [(cot * up * slope).astype(bf16), (cot * silu).astype(bf16)]
        proj = proj + jnp.sum(gate * grads[0].astype(f32) + up * grads[1].astype(f32), axis=1)
        grads = jnp.concatenate(grads, axis=1)
        pairs.append(lax.all_gather(grads, "width", axis=0, tiled=True))

    last = pairs[-1]
    w = lax.optimization_barrier(tied(gate_up, grads).reshape(width_here, 2 * units))
    proj = tied(proj, grads)
    rest = tied(part, grads)
    rest = lax.optimization_barrier((rest[0, n_head:], rest[1, n_head:]))
    rest = jnp.concatenate([p.astype(bf16) for p in rest], axis=1)

    lines = lax.axis_size("width")
    z = lax.axis_index("width")
    shared = jnp.zeros((lines, cap), f32)
    shared = lax.dynamic_update_slice_in_dim(shared, proj[None], z, 0)
    for shift in range(1, lines):
        ring = [(i, (i + shift) % lines) for i in range(lines)]
        got = lax.ppermute(proj, "width", ring)
        shared = lax.dynamic_update_slice_in_dim(shared, got[None], (z - shift) % lines, 0)
    for axis in ("batch", "hidden"):
        for step in bits(lax.axis_size(axis)):
            shared = shared + swap(shared, axis, step)

    pairs[0], shared, rest = lax.optimization_barrier((pairs[0], shared, rest))
    grad = None
    for c in range(chunks):
        grad = back(pairs[c], w, c, chunks, grad)

    groups = lax.axis_size("hidden")
    share = cap // groups
    grad = grad.reshape(count, groups, share, width_here)
    low = [("batch", step, 0) for step in bits(lax.axis_size("batch"))[:-1]]
    low += [("hidden", step, 1) for step in bits(groups)[:-1]]
    quad = ("batch", "hidden")
    for step in low:
        grad = halve(grad, *step)
    scaled = quad_sum(grad, quad) * gain
    start = lax.axis_index("hidden") * share
    unit = lax.dynamic_slice_in_dim(unit, start, share, 0)
    inv = lax.dynamic_slice_in_dim(inv_rms, start, share, 0)
    own = lax.axis_index("batch")
    proj = lax.dynamic_slice(shared, (own, start), (1, share))[0][:, None] / full_width
    grad = (scaled - unit * proj) * inv
    mine = (start + jnp.arange(share, dtype=jnp.int32) < audio_len[0])[:, None]
    grad = quad_spread(jnp.where(mine, grad, 0.0).astype(bf16), quad)
    for step in low[::-1]:
        grad = join(grad, *step)
    weight_grad = lax.dot_general(
        stack_all,
        grad.reshape(n_head, width_here),
        (((0,), (0,)), ((), ())),
        preferred_element_type=f32,
    )

    rest = lax.psum_scatter(tied(rest, last), "width", scatter_dimension=0, tiled=True)
    rest, weight_grad = lax.optimization_barrier((rest, weight_grad))
    _, up, _, silu = gates(rest.astype(f32))
    hidden_tail = (silu * up).astype(bf16)
    hidden = jnp.concatenate([jnp.concatenate(hidden_head, axis=1), hidden_tail], axis=0)
    return (hidden, weight_grad.reshape(4, feat_here, width_here))


def solution(mesh):
    return jax.shard_map(
        on_device,
        mesh=mesh,
        in_specs=(
            P("batch", None, "hidden"),
            P(None, "hidden", "width"),
            P("batch", "width"),
            P("batch"),
            P("batch"),
            P("width"),
            P("width", None, ("batch", "hidden")),
            P("width", ("batch", "hidden")),
        ),
        out_specs=(P("width", ("batch", "hidden")), P(None, "hidden", "width")),
        check_vma=False,
    )
```
